256 devices in a mesh: row: 16 (over z, x_lo), col: 16 (over y, x_hi, core).
Axes of the slice: x: 4 (x_hi: 2, x_lo: 2; x = x_hi * 2 + x_lo), y: 4, z: 8, core: 2. Of those that a mesh axis runs over, the one named last changes fastest.
Arguments:
- resident_inverse: float32 [12288, 12288], P('row', 'col'), as said below
- factor_panel: float32 [2, 12288, 256], P(None, 'row', 'col'), may hold values from -0.109375 to 0.109375
- diag_inverse: float32 [2, 256, 256], P(None, 'row', 'col'), as said below
- ancestors: int32 [2, 48], replicated, may hold values from 0 to 1, as said below
- start_order: int32 [2], replicated, may hold values from 0 to 1, each once
Outputs:
- inverse_column: float32 [2, 12288, 256], P(None, 'row', 'col')
- inverse_row: float32 [2, 256, 12288], P(None, 'row', 'col')
- diagonal_block: float32 [2, 256, 256], P(None, 'row', 'col')
The draws below stay inside these ranges and needn't reach their ends.
Inputs may be any that keep to these rules, and one draw needn't show every extreme that they name: `ancestors`: 1 marks a tile of 256 rows among the supernode's ancestor rows; each supernode marks between 32 and 48 tiles. `start_order`: a permutation of the supernodes. `resident_inverse`: symmetric. `diag_inverse`: each supernode's block is symmetric.
All inputs are finite; a program needn't handle non-finite values.
Results may differ from the reference program's by a relative error of at most 0.0001.
Values sent between devices are 32-bit elements; how exact they have to be, the bound alone decides.
A program may use at most 64 MiB of HBM per device.

```python
import math
import jax
import jax.numpy as jnp
from jax import lax

ORD = 12288
W = 256
TILE = 256
SUPER = 2
NT = 48


def draw_resident_inverse(key, part):
    off_key = jax.random.fold_in(key, 11)
    diag_key = jax.random.fold_in(key, 12)
    entries = jax.random.normal(off_key, (ORD, ORD), jnp.float32)
    symmetric = (entries + entries.T) * (0.70710678 / math.sqrt(ORD))
    diagonal = 3.0 + 2.0 * jax.random.uniform(diag_key, (ORD,), jnp.float32)
    positions = jnp.arange(ORD)
    return symmetric.at[positions, positions].set(diagonal)


def draw_diag_inverse(key, part):
    off_key = jax.random.fold_in(key, 21)
    diag_key = jax.random.fold_in(key, 22)
    entries = jax.random.normal(off_key, (SUPER, W, W), jnp.float32)
    symmetric = (entries + jnp.swapaxes(entries, 1, 2)) * (0.70710678 * 0.7 / math.sqrt(W))
    diagonal = 2.0 + 1.5 * jax.random.uniform(diag_key, (SUPER, W), jnp.float32)
    return symmetric + jnp.eye(W, dtype=jnp.float32)[None, :, :] * diagonal[:, :, None]


def draw_ancestors(key, part):
    count_key = jax.random.fold_in(key, 31)
    score_key = jax.random.fold_in(key, 32)
    counts = jax.random.randint(count_key, (SUPER, 1), 2 * NT // 3, NT + 1)
    noise = jax.random.randint(score_key, (SUPER, NT), 0, NT)
    tiles = jnp.arange(NT, dtype=jnp.int32)[None, :]
    scores = (noise + 2 * tiles) * NT + tiles
    ranking = jnp.argsort(jnp.argsort(-scores, axis=1), axis=1)
    return (ranking < counts).astype(jnp.int32)


def steps_of(stream_key, shape, shards, smallest, largest):
    def one(axis_at, blocks):
        heights = jax.random.uniform(jax.random.fold_in(jax.random.fold_in(stream_key, 6), axis_at), (blocks,), jnp.float32, smallest / len(shards), largest / len(shards))
        return jnp.repeat(jnp.exp(heights), shape[axis_at] // blocks).reshape((-1,) + (1,) * (len(shape) - axis_at - 1))

    loudness = one(*shards[0])
    for cut in shards[1:]:
        loudness = loudness * one(*cut)
    return loudness


def centred(key, dims, spread, bound, pieces=(), held_as=jnp.bfloat16):
    array = jax.random.normal(key, dims, jnp.float32) * spread
    if len(pieces) > 0:
        array = steps_of(key, dims, pieces, -0.22, 0.18) * array
    return jnp.clip(array, min=-bound, max=bound).astype(held_as)


def setup_inputs(seed: int = 0) -> dict:
    splits = jax.random.split(jax.random.key(seed), 6)
    resident_inverse = draw_resident_inverse(jax.random.fold_in(splits[5], 71), 0)
    factor_panel = centred(splits[1], (SUPER, ORD, W), (ORD // 4) ** -0.5, 0.109375, ((1, 16), (2, 16)), jnp.float32)
    diag_inverse = draw_diag_inverse(jax.random.fold_in(splits[5], 71), 0)
    ancestors = draw_ancestors(jax.random.fold_in(splits[5], 71), 0)
    start_order = jax.random.permutation(splits[4], SUPER).astype(jnp.int32)
    return dict(resident_inverse=resident_inverse, factor_panel=factor_panel, diag_inverse=diag_inverse, ancestors=ancestors, start_order=start_order)


def reference(resident_inverse, factor_panel, diag_inverse, ancestors, start_order):
    columns = []
    transposed_rows = []
    blocks = []
    for section_index in range(SUPER):
        chosen = start_order[section_index]
        tile_flags = jnp.repeat(ancestors[chosen], TILE).astype(jnp.float32)
        masked = factor_panel[chosen] * tile_flags[:, None]
        column = -tile_flags[:, None] * jnp.dot(resident_inverse, masked, precision=lax.Precision.HIGHEST)
        transposed = -jnp.dot(masked.T, resident_inverse, precision=lax.Precision.HIGHEST) * tile_flags[None, :]
        diagonal = diag_inverse[chosen] - jnp.dot(masked.T, column, precision=lax.Precision.HIGHEST)
        columns.append(column)
        transposed_rows.append(transposed)
        blocks.append(diagonal)
    return jnp.stack(columns), jnp.stack(transposed_rows), jnp.stack(blocks)
```

```python
import jax
import jax.numpy as jnp
from jax import lax
from jax.experimental import pallas as pl
from jax.experimental.pallas import tpu as pltpu
from jax.sharding import PartitionSpec as P

MESH = pl.DeviceIdType.MESH
TILE = 256
S = 2
NR = 16
NC = 16
NZ = 8
NY = 4
ROWS = 768
COLS = 768
N = 16
W = 256
CHIPS = [(dy, dx) for dy in (0, 1, 3, 2) for dx in (0, 1) if (dy, dx) != (0, 0)]
BF = jnp.bfloat16
F32 = jnp.float32


def split(x):
    hi = x.astype(BF)
    lo = (x - hi.astype(F32)).astype(BF)
    return hi, lo


def chain_length(s, d):
    return NZ // 2 if (s == 0) == (d == 1) else NZ // 2 - 1


def kernel(
    anc, order, a_hbm, p_ref, dinv_ref,
    row_ref, col_ref, diag_ref,
    a_buf, a_hi, a_lo, mine, pt, t, rp, f, xr, m, mpad, dp, dr,
    a_sem, ag_send, ag_recv, sib_send, sib_recv, fw_send, fw_recv,
    rs_send, rs_recv, x_send, x_recv, m_send, m_recv, d_send, d_recv,
):
    r = lax.axis_index("row")
    c = lax.axis_index("col")
    z, xl = r // 2, r % 2
    y, xh, k = c // 4, (c // 2) % 2, c % 2
    off_diagonal = r != c

    def col_at(dy, dx, core):
        return ((y + dy) % NY) * 4 + ((xh + dx) % 2) * 2 + core

    def row_at(dz, dx):
        return ((z + dz) % NZ) * 2 + (xl + dx) % 2

    sibling = (r, col_at(0, 0, 1 - k))
    x_peer = (row_at(0, 1), c)
    row_peers = [(j // 2, j % 2) for j in range(1, NR)]

    a_copy = pltpu.make_async_copy(a_hbm, a_buf, a_sem)
    a_copy.start()

    barrier = pltpu.get_barrier_semaphore()

    def greet(device):
        pl.semaphore_signal(barrier, inc=1, device_id=device, device_id_type=MESH)

    greet(sibling)
    for dy, dx in CHIPS:
        greet((r, col_at(dy, dx, k)))
    for dz, dx in row_peers:
        greet((row_at(dz, dx), c))

    @pl.when(off_diagonal)
    def _():
        greet((c, r))

    def flag(s, tile):
        return anc[order[s], tile].astype(F32)

    first = order[0] == 0
    for s in range(S):
        chosen = jnp.where(first, p_ref[s], p_ref[1 - s])
        for b in range(ROWS // TILE):
            here = pl.ds(b * TILE, TILE)
            mine[s, :, here] = chosen[:, b * TILE : (b + 1) * TILE] * flag(s, r * 3 + b)

    pl.semaphore_wait(barrier, 1 + len(CHIPS) + len(row_peers) + off_diagonal.astype(jnp.int32))

    def remote(src, dst, send, recv, device):
        return pltpu.make_async_remote_copy(
            src_ref=src, dst_ref=dst, send_sem=send, recv_sem=recv, device_id=device, device_id_type=MESH
        )

    sent = []
    for s in range(S):
        for i, (dy, dx) in enumerate(CHIPS):
            copy = remote(mine.at[s], pt.at[s, c], ag_send.at[s, i], ag_recv.at[s, i], (r, col_at(dy, dx, k)))
            copy.start()
            sent.append(copy)
        copy = remote(mine.at[s], pt.at[s, c], sib_send.at[s], sib_recv.at[s], sibling)
        copy.start()
        sent.append(copy)
        pt[s, c] = mine[s]

    a_copy.wait()
    for b in range(3):
        here = pl.ds(b * TILE, TILE)
        hi, lo = split(a_buf[here, :])
        a_hi[here, :] = hi
        a_lo[here, :] = lo

    def gathered(s):
        for i, (dy, dx) in enumerate(CHIPS):
            slot = col_at(-dy, dx, k)
            remote(mine.at[s], pt.at[s, slot], ag_send.at[s, i], ag_recv.at[s, i], sibling).wait_recv()
            copy = remote(pt.at[s, slot], pt.at[s, slot], fw_send.at[s, i], fw_recv.at[s, i], sibling)
            copy.start()
            sent.append(copy)
        other = col_at(0, 0, 1 - k)
        remote(mine.at[s], pt.at[s, other], sib_send.at[s], sib_recv.at[s], sibling).wait_recv()
        for i, (dy, dx) in enumerate(CHIPS):
            slot = col_at(-dy, dx, 1 - k)
            remote(mine.at[s], pt.at[s, slot], fw_send.at[s, i], fw_recv.at[s, i], sibling).wait_recv()

    def multiply(s):
        hi, lo = split(pt[s].reshape(W, ROWS))

        for b in range(3):
            here = pl.ds(b * TILE, TILE)
            u, v = a_hi[:, here], a_lo[:, here]
            total = jnp.dot(hi, u, preferred_element_type=F32)
            total += jnp.dot(hi, v, preferred_element_type=F32)
            total += jnp.dot(lo, u, preferred_element_type=F32)
            t[s, :, :, here] = total.reshape(NZ, 32, TILE)

    def hop(s, d, j):
        length = chain_length(s, d)
        e = 0 if d == 1 else 1
        target = (z + d * (length - j)) % NZ
        if j == 0:
            src = t.at[s, target]
        else:
            arrived(s, d, j - 1)
            src = rp.at[s, e, j - 1]
            src[...] += t[s, target]
        copy = remote(src, rp.at[s, e, j], rs_send.at[s, e, j], rs_recv.at[s, e, j], (row_at(d, 0), c))
        copy.start()
        sent.append(copy)

    def arrived(s, d, j):
        e = 0 if d == 1 else 1
        remote(t.at[s, 0], rp.at[s, e, j], rs_send.at[s, e, j], rs_recv.at[s, e, j], x_peer).wait_recv()

    for s in range(S):
        gathered(s)
        multiply(s)
        for d in (1, -1):
            hop(s, d, 0)
    for j in range(1, NZ // 2):
        for s in range(S):
            for d in (1, -1):
                if j < chain_length(s, d):
                    hop(s, d, j)

    for s in range(S):
        ends = [chain_length(s, d) - 1 for d in (1, -1)]
        arrived(s, 1, ends[0])
        arrived(s, -1, ends[1])
        f[s] = (t[s, z] + rp[s, 0, ends[0]] + rp[s, 1, ends[1]]).reshape(2, N, COLS)
        copy = remote(f.at[s, 1 - xl], xr.at[s], x_send.at[s], x_recv.at[s], x_peer)
        copy.start()
        sent.append(copy)

    mpad[...] = jnp.zeros_like(mpad)
    for s in range(S):
        remote(f.at[s, 0], xr.at[s], x_send.at[s], x_recv.at[s], x_peer).wait_recv()
        for b in range(COLS // TILE):
            here = pl.ds(b * TILE, TILE)
            row_ref[s, :, here] = (f[s, xl, :, here] + xr[s, :, here]) * -flag(s, c * 3 + b)

        @pl.when(off_diagonal)
        def _(s=s):
            remote(row_ref.at[s], m.at[s], m_send.at[s], m_recv.at[s], (c, r)).start()

        @pl.when(jnp.logical_not(off_diagonal))
        def _(s=s):
            m[s] = row_ref[s]

    total = jnp.zeros((W, 128), F32)
    for s in range(S):

        @pl.when(off_diagonal)
        def _(s=s):
            remote(row_ref.at[s], m.at[s], m_send.at[s], m_recv.at[s], (c, r)).wait_recv()

        col_ref[s] = m[s]
        mpad[s, pl.ds(s * N, N), :] = m[s]
        hi, lo = split(pt[s].reshape(W, ROWS))
        u, v = split(mpad[s])
        for left, right in ((hi, u), (hi, v), (lo, u)):
            total += lax.dot_general(left, right, (((1,), (1,)), ((), ())), preferred_element_type=F32)
    halves = total.reshape(NR, 2, 8, 128)
    dp[...] = halves[:, 0] + pltpu.roll(halves[:, 1].reshape(NR * 8, 128), 32, 1).reshape(NR, 8, 128)
    for i, (dz, dx) in enumerate(row_peers):
        to = row_at(dz, dx)
        copy = remote(dp.at[to], dr.at[i], d_send.at[i], d_recv.at[i], (to, c))
        copy.start()
        sent.append(copy)
    summed = dp[r]
    for i in range(NR - 1):
        remote(dp.at[0], dr.at[i], d_send.at[i], d_recv.at[i], x_peer).wait_recv()
        summed += dr[i]
    for s in range(S):
        chosen = jnp.where(first, dinv_ref[s], dinv_ref[1 - s])
        for h in range(2):
            at = h * 32 + s * N
            diag_ref[s, pl.ds(h * 8, 8), :] = chosen[h * 8 : h * 8 + 8] - summed[:, at : at + N]

    for copy in sent:
        copy.wait_send()
    for s in range(S):

        @pl.when(off_diagonal)
        def _(s=s):
            remote(row_ref.at[s], m.at[s], m_send.at[s], m_recv.at[s], (c, r)).wait_send()


def on_device(resident_inverse, factor_panel, diag_inverse, ancestors, start_order):
    vmem = pl.BlockSpec(memory_space=pltpu.VMEM)
    smem = pl.BlockSpec(memory_space=pltpu.SMEM)
    dma = pltpu.SemaphoreType.DMA
    half = NZ // 2
    chips = len(CHIPS)
    row, col, diag = pl.pallas_call(
        kernel,
        out_shape=(
            jax.ShapeDtypeStruct((S, N, COLS), F32),
            jax.ShapeDtypeStruct((S, N, ROWS), F32),
            jax.ShapeDtypeStruct((S, N, N), F32),
        ),
        in_specs=[smem, smem, pl.BlockSpec(memory_space=pl.ANY), vmem, vmem],
        out_specs=(vmem, vmem, vmem),
        scratch_shapes=[
            pltpu.VMEM((ROWS, COLS), F32),
            pltpu.VMEM((ROWS, COLS), BF),
            pltpu.VMEM((ROWS, COLS), BF),
            pltpu.VMEM((S, N, ROWS), F32),
            pltpu.VMEM((S, NC, N, ROWS), F32),
            pltpu.VMEM((S, NZ, 2 * N, COLS), F32),
            pltpu.VMEM((S, 2, half, 2 * N, COLS), F32),
            pltpu.VMEM((S, 2, N, COLS), F32),
            pltpu.VMEM((S, N, COLS), F32),
            pltpu.VMEM((S, N, ROWS), F32),
            pltpu.VMEM((S, 128, ROWS), F32),
            pltpu.VMEM((NR, 8, 128), F32),
            pltpu.VMEM((NR - 1, 8, 128), F32),
            dma,
            dma((S, chips)),
            dma((S, chips)),
            dma((S,)),
            dma((S,)),
            dma((S, chips)),
            dma((S, chips)),
            dma((S, 2, half)),
            dma((S, 2, half)),
            dma((S,)),
            dma((S,)),
            dma((S,)),
            dma((S,)),
            dma((NR - 1,)),
            dma((NR - 1,)),
        ],
        compiler_params=pltpu.CompilerParams(
            collective_id=0, has_side_effects=True, vmem_limit_bytes=48 * 1024 * 1024
        ),
        name="selected_inverse",
    )(ancestors, start_order, resident_inverse, jnp.swapaxes(factor_panel, 1, 2), diag_inverse)
    return jnp.swapaxes(col, 1, 2), row, diag


def solution(mesh):
    return jax.shard_map(
        on_device,
        mesh=mesh,
        in_specs=(P("row", "col"), P(None, "row", "col"), P(None, "row", "col"), P(), P()),
        out_specs=(P(None, "row", "col"), P(None, "row", "col"), P(None, "row", "col")),
        check_vma=False,
    )
```

```python
import jax
import jax.numpy as jnp
from jax import lax
from jax.experimental import pallas as pl
from jax.experimental.pallas import tpu as pltpu
from jax.sharding import PartitionSpec as P

MESH = pl.DeviceIdType.MESH
BF = jnp.bfloat16
F32 = jnp.float32
TILE = 256
S = 2
U = 4
NR = 16
NC = 16
NZ = 8
NY = 4
ROWS = 768
COLS = 768
TILES = ROWS // TILE
N = 16
H = 8
W = NC * H
CHIPS = [(2, 1), (1, 1), (3, 1), (2, 0), (0, 1), (1, 0), (3, 0)]
CHAINS = [(1, 0), (-1, 1), (-1, 0), (1, 1)]
ROW_PEERS = sorted(((j // 2, j % 2) for j in range(1, NR)), key=lambda p: -min(p[0], NZ - p[0]) - p[1])


def split(x):
    hi = x.astype(BF)
    lo = (x - hi.astype(F32)).astype(BF)
    return hi, lo


def hops(d, g):
    return NZ // 2 if (d == 1) == (g == 0) else NZ // 2 - 1


def kernel(
    order_hbm, anc_hbm, a_hbm, p_hbm, dinv_hbm,
    row_ref, col_ref, diag_ref,
    order, anc, a_buf, a_hi, a_lo, dinv, pt, p_hi, p_lo, t, rp, fin, xr, rows, m, dp, dr,
    local_sem, ag_send, ag_recv, sib_send, sib_recv, fw_send, fw_recv,
    rs_send, rs_recv, fin_recv, x_send, x_recv, m_send, m_recv, d_send, d_recv,
):
    r = lax.axis_index("row")
    c = lax.axis_index("col")
    z, xl = r // 2, r % 2
    y, xh, k = c // 4, (c // 2) % 2, c % 2
    off_diagonal = r != c

    def col_at(dy, dx, core):
        return ((y + dy) % NY) * 4 + ((xh + dx) % 2) * 2 + core

    def row_at(dz, dx):
        return ((z + dz) % NZ) * 2 + (xl + dx) % 2

    sibling = (r, col_at(0, 0, 1 - k))
    x_peer = (row_at(0, 1), c)
    barrier = pltpu.get_barrier_semaphore()
    greeted = [(r, col_at(dy, dx, k)) for dy, dx in CHIPS]
    greeted += [(row_at(1, 0), c), (row_at(-1, 0), c), (row_at(1, 1), c), (row_at(-1, 1), c), x_peer, sibling]
    for device in greeted:
        pl.semaphore_signal(barrier, inc=1, device_id=device, device_id_type=MESH)

    locals_ = [
        pltpu.make_async_copy(a_hbm, a_buf, local_sem.at[0]),
        pltpu.make_async_copy(anc_hbm, anc, local_sem.at[1]),
        pltpu.make_async_copy(order_hbm, order, local_sem.at[2]),
        pltpu.make_async_copy(dinv_hbm, dinv, local_sem.at[3]),
    ]
    for u in range(U):
        mine = p_hbm.at[u // 2, pl.ds(u % 2 * H, H)]
        locals_.append(pltpu.make_async_copy(mine, pt.at[u, c], local_sem.at[4 + u]))
    for copy in locals_:
        copy.start()
    pl.semaphore_wait(barrier, len(greeted))

    sent = []

    def remote(src, dst, send, recv, device):
        return pltpu.make_async_remote_copy(
            src_ref=src, dst_ref=dst, send_sem=send, recv_sem=recv, device_id=device, device_id_type=MESH
        )

    def send(*args):
        copy = remote(*args)
        copy.start()
        sent.append(copy)

    def spread(u):
        mine = p_hbm.at[u // 2, pl.ds(u % 2 * H, H)]
        for i, (dy, dx) in enumerate(CHIPS):
            send(mine, pt.at[u, c], ag_send.at[u, i], ag_recv.at[u, i], (r, col_at(dy, dx, k)))
        send(mine, pt.at[u, c], sib_send.at[u], sib_recv.at[u], sibling)

    def forward(u):
        for i, (dy, dx) in list(enumerate(CHIPS))[::-1]:
            slot = col_at(-dy, dx, k)
            remote(pt.at[u, slot], pt.at[u, slot], ag_send.at[u, i], ag_recv.at[u, i], sibling).wait_recv()
            send(pt.at[u, slot], pt.at[u, slot], fw_send.at[u, i], fw_recv.at[u, i], sibling)

    def multiply(u):
        locals_[4 + u].wait()
        other = col_at(0, 0, 1 - k)
        remote(pt.at[u, other], pt.at[u, other], sib_send.at[u], sib_recv.at[u], sibling).wait_recv()
        for i, (dy, dx) in enumerate(CHIPS):
            slot = col_at(-dy, dx, 1 - k)
            remote(pt.at[u, slot], pt.at[u, slot], fw_send.at[u, i], fw_recv.at[u, i], sibling).wait_recv()
        for b in range(TILES):
            here = pl.ds(b * TILE, TILE)
            flag = anc[u // 2, r * TILES + b].astype(F32)
            hi, lo = split(pt[u, :, :, here].reshape(W, TILE) * flag)
            p_hi[u, :, here] = hi
            p_lo[u, :, here] = lo
        for b in range(TILES):
            here = pl.ds(b * TILE, TILE)
            v, w = a_hi[:, here], a_lo[:, here]
            total = jnp.dot(p_hi[u], v, preferred_element_type=F32)
            total += jnp.dot(p_hi[u], w, preferred_element_type=F32)
            total += jnp.dot(p_lo[u], v, preferred_element_type=F32)
            t[u, :, :, :, here] = total.reshape(NZ, 2, H, TILE)

    def side(d):
        return 0 if d == 1 else 1

    def hop(u, j):
        for d, g in CHAINS:
            last = hops(d, g) - 1
            if j > last:
                continue
            e = side(d)
            block = t.at[u, (z + d * (last + 1 - j)) % NZ, (xl + g) % 2]
            if j == 0:
                src = block
            else:
                src = rp.at[u, e, g, j - 1]
                remote(src, src, rs_send.at[u, e, g, j - 1], rs_recv.at[u, e, g, j - 1], x_peer).wait_recv()
                src[...] += block[...]
            if j == last:
                send(src, fin.at[u, e, g], rs_send.at[u, e, g, j], fin_recv.at[u, e, g], (row_at(d, g), c))
            else:
                send(src, rp.at[u, e, g, j], rs_send.at[u, e, g, j], rs_recv.at[u, e, g, j], (row_at(d, 0), c))
        if j == 0:
            send(t.at[u, z, 1 - xl], xr.at[u], x_send.at[u], x_recv.at[u], x_peer)

    def mirror(u):
        there = m.at[u // 2, pl.ds(u % 2 * H, H)]
        return remote(rows.at[u], there, m_send.at[u], m_recv.at[u], (c, r))

    def finish(u):
        remote(xr.at[u], xr.at[u], x_send.at[u], x_recv.at[u], x_peer).wait_recv()
        for d, g in CHAINS[2:] + CHAINS[:2]:
            e = side(d)
            there = fin.at[u, e, g]
            remote(there, there, rs_send.at[u, e, g, 0], fin_recv.at[u, e, g], x_peer).wait_recv()
        for b in range(TILES):
            here = pl.ds(b * TILE, TILE)
            total = t[u, z, xl, :, here] + xr[u, :, here]
            total += fin[u, 0, 0, :, here] + fin[u, 0, 1, :, here]
            total += fin[u, 1, 0, :, here] + fin[u, 1, 1, :, here]
            rows[u, :, here] = total * -anc[u // 2, c * TILES + b].astype(F32)

        @pl.when(off_diagonal)
        def _():
            mirror(u).start()

        @pl.when(jnp.logical_not(off_diagonal))
        def _():
            m[u // 2, pl.ds(u % 2 * H, H), :] = rows[u]

    def diagonal(s):
        for h in range(2):

            @pl.when(off_diagonal)
            def _():
                mirror(2 * s + h).wait_recv()

        v, w = split(m[s])
        halves = []
        for h in range(2):
            total = jnp.zeros((W, 128), F32)
            for left, right in ((p_hi, v), (p_hi, w), (p_lo, v)):
                total += lax.dot_general(
                    left[2 * s + h], right, (((1,), (1,)), ((), ())), preferred_element_type=F32
                )
            halves.append(total)
        dp[s] = (halves[0] + pltpu.roll(halves[1], N, 1)).reshape(NR, 8, 128)
        for i, (dz, dx) in enumerate(ROW_PEERS):
            to = row_at(dz, dx)
            send(dp.at[s, to], dr.at[s, i], d_send.at[s, i], d_recv.at[s, i], (to, c))

    def add_diagonal(s):
        total = dp[s, r]
        for i in list(range(NR - 1))[::-1]:
            remote(dr.at[s, i], dr.at[s, i], d_send.at[s, i], d_recv.at[s, i], x_peer).wait_recv()
            total += dr[s, i]
        return total

    spread(0)
    m[:, pl.ds(N, 128 - N), :] = jnp.zeros((S, 128 - N, ROWS), F32)
    locals_[0].wait()
    for b in range(TILES):
        here = pl.ds(b * TILE, TILE)
        hi, lo = split(a_buf[here, :])
        a_hi[here, :] = hi
        a_lo[here, :] = lo
    locals_[1].wait()
    spread(1)
    forward(0)
    spread(2)
    multiply(0)
    hop(0, 0)
    forward(1)
    spread(3)
    multiply(1)
    hop(1, 0)
    hop(0, 1)
    forward(2)
    multiply(2)
    hop(2, 0)
    hop(1, 1)
    hop(0, 2)
    forward(3)
    multiply(3)
    hop(3, 0)
    hop(2, 1)
    hop(1, 2)
    hop(0, 3)
    hop(3, 1)
    hop(2, 2)
    hop(1, 3)
    finish(0)
    hop(3, 2)
    hop(2, 3)
    finish(1)
    hop(3, 3)
    finish(2)
    finish(3)
    diagonal(0)
    diagonal(1)
    for copy in locals_[2:4]:
        copy.wait()
    in_place = order[0] == 0
    for s in range(S):
        col_ref[s] = jnp.where(in_place, m[s, pl.ds(0, N), :], m[1 - s, pl.ds(0, N), :])
        for h in range(2):
            row_ref[s, pl.ds(h * H, H), :] = jnp.where(in_place, rows[2 * s + h], rows[2 - 2 * s + h])
    totals = [add_diagonal(s) for s in range(S)]
    for s in range(S):
        total = jnp.where(in_place, totals[s], totals[1 - s])
        for h in range(2):
            chosen = jnp.where(in_place, dinv[s, pl.ds(h * H, H)], dinv[1 - s, pl.ds(h * H, H)])
            diag_ref[s, pl.ds(h * H, H), :] = chosen - total[:, h * N : (h + 1) * N]
    for copy in sent:
        copy.wait_send()
    for u in range(U):

        @pl.when(off_diagonal)
        def _(u=u):
            mirror(u).wait_send()


def on_device(resident_inverse, factor_panel, diag_inverse, ancestors, start_order):
    vmem = pl.BlockSpec(memory_space=pltpu.VMEM)
    hbm = pl.BlockSpec(memory_space=pltpu.HBM)
    dma = pltpu.SemaphoreType.DMA
    half = NZ // 2
    chips = len(CHIPS)
    row, col, diag = pl.pallas_call(
        kernel,
        out_shape=(
            jax.ShapeDtypeStruct((S, N, COLS), F32),
            jax.ShapeDtypeStruct((S, N, ROWS), F32),
            jax.ShapeDtypeStruct((S, N, N), F32),
        ),
        in_specs=[hbm] * 5,
        out_specs=(vmem, vmem, vmem),
        scratch_shapes=[
            pltpu.SMEM(start_order.shape, jnp.int32),
            pltpu.SMEM(ancestors.shape, jnp.int32),
            pltpu.VMEM((ROWS, COLS), F32),
            pltpu.VMEM((ROWS, COLS), BF),
            pltpu.VMEM((ROWS, COLS), BF),
            pltpu.VMEM((S, N, N), F32),
            pltpu.VMEM((U, NC, H, ROWS), F32),
            pltpu.VMEM((U, W, ROWS), BF),
            pltpu.VMEM((U, W, ROWS), BF),
            pltpu.VMEM((U, NZ, 2, H, COLS), F32),
            pltpu.VMEM((U, 2, 2, half - 1, H, COLS), F32),
            pltpu.VMEM((U, 2, 2, H, COLS), F32),
            pltpu.VMEM((U, H, COLS), F32),
            pltpu.VMEM((U, H, COLS), F32),
            pltpu.VMEM((S, 128, ROWS), F32),
            pltpu.VMEM((S, NR, 8, 128), F32),
            pltpu.VMEM((S, NR - 1, 8, 128), F32),
            dma((8,)),
            dma((U, chips)),
            dma((U, chips)),
            dma((U,)),
            dma((U,)),
            dma((U, chips)),
            dma((U, chips)),
            dma((U, 2, 2, half)),
            dma((U, 2, 2, half - 1)),
            dma((U, 2, 2)),
            dma((U,)),
            dma((U,)),
            dma((U,)),
            dma((U,)),
            dma((S, NR - 1)),
            dma((S, NR - 1)),
        ],
        compiler_params=pltpu.CompilerParams(
            collective_id=0, has_side_effects=True, vmem_limit_bytes=60 * 1024 * 1024
        ),
        name="selected_inverse",
    )(start_order, ancestors, resident_inverse, jnp.swapaxes(factor_panel, 1, 2), diag_inverse)
    return jnp.swapaxes(col, 1, 2), row, diag


def solution(mesh):
    return jax.shard_map(
        on_device,
        mesh=mesh,
        in_specs=(P("row", "col"), P(None, "row", "col"), P(None, "row", "col"), P(), P()),
        out_specs=(P(None, "row", "col"), P(None, "row", "col"), P(None, "row", "col")),
        check_vma=False,
    )
```

```python
import jax
import jax.numpy as jnp
from jax import lax
from jax.experimental import pallas as pl
from jax.experimental.pallas import tpu as pltpu
from jax.sharding import PartitionSpec as P

MESH = pl.DeviceIdType.MESH
BF = jnp.bfloat16
F32 = jnp.float32
TILE = 256
S = 2
U = 4
NR = 16
NC = 16
NZ = 8
NY = 4
ROWS = 768
COLS = 768
TILES = ROWS // TILE
N = 16
H = 8
W = NC * H
CHIPS = [(2, 1), (1, 1), (3, 1), (2, 0), (0, 1), (1, 0), (3, 0)]
CHAINS = [(1, 0), (-1, 1), (-1, 0), (1, 1)]
ROW_PEERS = sorted(((j // 2, j % 2) for j in range(1, NR)), key=lambda p: -min(p[0], NZ - p[0]) - p[1])


def split(x):
    hi = x.astype(BF)
    lo = (x - hi.astype(F32)).astype(BF)
    return hi, lo


def hops(d, g):
    return NZ // 2 if (d == 1) == (g == 0) else NZ // 2 - 1


def kernel(
    order_hbm, anc_hbm, a_hbm, p_hbm, dinv_hbm,
    row_ref, col_ref, diag_ref,
    order, anc, a_buf, a_hi, a_lo, dinv, outs, diags, pt, p_hi, p_lo, t, rp, fin, xr, rows, m, dp, dr,
    local_sem, out_sem, ag_send, ag_recv, sib_send, sib_recv, fw_send,
    rs_send, rs_recv, fin_recv, x_send, x_recv, m_send, m_recv, d_send, d_recv,
):
    r = lax.axis_index("row")
    c = lax.axis_index("col")
    z, xl = r // 2, r % 2
    y, xh, k = c // 4, (c // 2) % 2, c % 2
    off_diagonal = r != c

    def col_at(dy, dx, core):
        return ((y + dy) % NY) * 4 + ((xh + dx) % 2) * 2 + core

    def row_at(dz, dx):
        return ((z + dz) % NZ) * 2 + (xl + dx) % 2

    sibling = (r, col_at(0, 0, 1 - k))
    x_peer = (row_at(0, 1), c)
    barrier = pltpu.get_barrier_semaphore()
    greeted = [(r, col_at(dy, dx, k)) for dy, dx in CHIPS]
    greeted += [(row_at(1, 0), c), (row_at(-1, 0), c), (row_at(1, 1), c), (row_at(-1, 1), c), x_peer, sibling]
    for device in greeted:
        pl.semaphore_signal(barrier, inc=1, device_id=device, device_id_type=MESH)

    locals_ = [
        pltpu.make_async_copy(a_hbm, a_buf, local_sem.at[0]),
        pltpu.make_async_copy(anc_hbm, anc, local_sem.at[1]),
        pltpu.make_async_copy(order_hbm, order, local_sem.at[2]),
        pltpu.make_async_copy(dinv_hbm, dinv, local_sem.at[3]),
    ]
    for u in range(U):
        mine = p_hbm.at[u // 2, pl.ds(u % 2 * H, H)]
        locals_.append(pltpu.make_async_copy(mine, pt.at[u, c], local_sem.at[4 + u]))
    for copy in locals_:
        copy.start()
    pl.semaphore_wait(barrier, len(greeted))

    sent = []

    def remote(src, dst, send, recv, device):
        return pltpu.make_async_remote_copy(
            src_ref=src, dst_ref=dst, send_sem=send, recv_sem=recv, device_id=device, device_id_type=MESH
        )

    def send(*args):
        copy = remote(*args)
        copy.start()
        sent.append(copy)

    def settle():
        for copy in sent:
            copy.wait_send()
        sent.clear()

    def spread(u):
        mine = p_hbm.at[u // 2, pl.ds(u % 2 * H, H)]
        for i, (dy, dx) in enumerate(CHIPS):
            send(mine, pt.at[u, c], ag_send.at[u, i], ag_recv.at[u, i], (r, col_at(dy, dx, k)))
        send(mine, pt.at[u, c], sib_send.at[u], sib_recv.at[u], sibling)

    def forward(u):
        for i, (dy, dx) in list(enumerate(CHIPS))[::-1]:
            slot = col_at(-dy, dx, k)
            remote(pt.at[u, slot], pt.at[u, slot], ag_send.at[u, i], ag_recv.at[u, i], sibling).wait_recv()
            send(pt.at[u, slot], pt.at[u, slot], fw_send.at[u, i], sib_recv.at[u], sibling)

    def multiply(u):
        locals_[4 + u].wait()
        half = pt.at[u, pl.ds(0, NC // 2)]
        remote(half, half, sib_send.at[u], sib_recv.at[u], sibling).wait_recv()
        for b in range(TILES):
            here = pl.ds(b * TILE, TILE)
            flag = anc[u // 2, r * TILES + b].astype(F32)
            hi, lo = split(pt[u, :, :, here].reshape(W, TILE) * flag)
            p_hi[u, :, here] = hi
            p_lo[u, :, here] = lo
        for b in range(TILES):
            here = pl.ds(b * TILE, TILE)
            v, w = a_hi[:, here], a_lo[:, here]
            total = jnp.dot(p_hi[u], v, preferred_element_type=F32)
            total += jnp.dot(p_hi[u], w, preferred_element_type=F32)
            total += jnp.dot(p_lo[u], v, preferred_element_type=F32)
            t[u, :, :, :, here] = total.reshape(NZ, 2, H, TILE)

    def side(d):
        return 0 if d == 1 else 1

    def hop(u, j):
        for d, g in CHAINS:
            last = hops(d, g) - 1
            if j > last:
                continue
            e = side(d)
            block = t.at[u, (z + d * (last + 1 - j)) % NZ, (xl + g) % 2]
            if j == 0:
                src = block
            else:
                src = rp.at[u, e, g, j - 1]
                remote(src, src, rs_send.at[u, e, g, j - 1], rs_recv.at[u, e, g, j - 1], x_peer).wait_recv()
                src[...] += block[...]
            if j == last:
                send(src, fin.at[u, e, g], rs_send.at[u, e, g, j], fin_recv.at[u, e, g], (row_at(d, g), c))
            else:
                send(src, rp.at[u, e, g, j], rs_send.at[u, e, g, j], rs_recv.at[u, e, g, j], (row_at(d, 0), c))
        if j == 0:
            send(t.at[u, z, 1 - xl], xr.at[u], x_send.at[u], x_recv.at[u], x_peer)

    def mirror(u):
        there = m.at[u // 2, pl.ds(u % 2 * H, H)]
        return remote(rows.at[u], there, m_send.at[u], m_recv.at[u], (c, r))

    def finish(u):
        remote(xr.at[u], xr.at[u], x_send.at[u], x_recv.at[u], x_peer).wait_recv()
        for d, g in CHAINS[2:] + CHAINS[:2]:
            e = side(d)
            there = fin.at[u, e, g]
            remote(there, there, rs_send.at[u, e, g, 0], fin_recv.at[u, e, g], x_peer).wait_recv()
        for b in range(TILES):
            here = pl.ds(b * TILE, TILE)
            total = t[u, z, xl, :, here] + xr[u, :, here]
            total += fin[u, 0, 0, :, here] + fin[u, 0, 1, :, here]
            total += fin[u, 1, 0, :, here] + fin[u, 1, 1, :, here]
            rows[u, :, here] = total * -anc[u // 2, c * TILES + b].astype(F32)

        @pl.when(off_diagonal)
        def _():
            mirror(u).start()

        @pl.when(jnp.logical_not(off_diagonal))
        def _():
            m[u // 2, pl.ds(u % 2 * H, H), :] = rows[u]

    def diagonal(s):
        for h in range(2):

            @pl.when(off_diagonal)
            def _():
                mirror(2 * s + h).wait_recv()

        v, w = split(m[s])
        halves = []
        for h in range(2):
            total = jnp.zeros((W, 128), F32)
            for left, right in ((p_hi, v), (p_hi, w), (p_lo, v)):
                total += lax.dot_general(
                    left[2 * s + h], right, (((1,), (1,)), ((), ())), preferred_element_type=F32
                )
            halves.append(total)
        dp[s] = (halves[0] + pltpu.roll(halves[1], N, 1)).reshape(NR, 8, 128)
        for i, (dz, dx) in enumerate(ROW_PEERS):
            to = row_at(dz, dx)
            send(dp.at[s, to], dr.at[s, i], d_send.at[s, i], d_recv.at[s], (to, c))

    def add_diagonal(s):
        total = dp[s, r]
        remote(dr.at[s], dr.at[s], d_send.at[s, 0], d_recv.at[s], x_peer).wait_recv()
        for i in range(NR - 1):
            total += dr[s, i]
        return total

    spread(0)
    m[:, pl.ds(N, 128 - N), :] = jnp.zeros((S, 128 - N, ROWS), F32)
    locals_[0].wait()
    for b in range(TILES):
        here = pl.ds(b * TILE, TILE)
        hi, lo = split(a_buf[here, :])
        a_hi[here, :] = hi
        a_lo[here, :] = lo
    locals_[1].wait()
    spread(1)
    forward(0)
    spread(2)
    multiply(0)
    hop(0, 0)
    forward(1)
    spread(3)
    multiply(1)
    hop(1, 0)
    hop(0, 1)
    forward(2)
    multiply(2)
    hop(2, 0)
    hop(1, 1)
    hop(0, 2)
    forward(3)
    multiply(3)
    hop(3, 0)
    hop(2, 1)
    hop(1, 2)
    hop(0, 3)
    hop(3, 1)
    hop(2, 2)
    hop(1, 3)
    finish(0)
    hop(3, 2)
    hop(2, 3)
    finish(1)
    hop(3, 3)
    finish(2)
    finish(3)
    settle()
    diagonal(0)
    diagonal(1)
    for u in range(U):

        @pl.when(off_diagonal)
        def _(u=u):
            mirror(u).wait_send()

    for copy in locals_[2:4]:
        copy.wait()
    in_place = order[0] == 0
    for s in range(S):
        outs[0, s] = jnp.where(in_place, m[s, pl.ds(0, N), :], m[1 - s, pl.ds(0, N), :])
        for h in range(2):
            outs[1, s, pl.ds(h * H, H), :] = jnp.where(in_place, rows[2 * s + h], rows[2 - 2 * s + h])
    stores = [
        pltpu.make_async_copy(outs.at[0], col_ref, out_sem.at[0]),
        pltpu.make_async_copy(outs.at[1], row_ref, out_sem.at[1]),
        pltpu.make_async_copy(diags, diag_ref, out_sem.at[2]),
    ]
    stores[0].start()
    stores[1].start()
    settle()
    totals = [add_diagonal(s) for s in range(S)]
    for s in range(S):
        total = jnp.where(in_place, totals[s], totals[1 - s])
        for h in range(2):
            chosen = jnp.where(in_place, dinv[s, pl.ds(h * H, H)], dinv[1 - s, pl.ds(h * H, H)])
            diags[s, pl.ds(h * H, H), :] = chosen - total[:, h * N : (h + 1) * N]
    stores[2].start()
    for copy in stores:
        copy.wait()


def copy_out(*refs):
    for i in range(3):
        refs[3 + i][...] = refs[i][...]


def deliver(*arrays):
    return pl.pallas_call(
        copy_out,
        out_shape=tuple(jax.ShapeDtypeStruct(x.shape, x.dtype) for x in arrays),
        in_specs=[pl.BlockSpec(memory_space=pltpu.VMEM)] * 3,
        out_specs=(pl.BlockSpec(memory_space=pltpu.VMEM),) * 3,
        scratch_shapes=[pltpu.VMEM(x.shape, x.dtype) for x in arrays] + [pltpu.SemaphoreType.DMA((6,))],
        name="deliver",
    )(*arrays)


def on_device(resident_inverse, factor_panel, diag_inverse, ancestors, start_order):
    hbm = pl.BlockSpec(memory_space=pltpu.HBM)
    dma = pltpu.SemaphoreType.DMA
    half = NZ // 2
    chips = len(CHIPS)
    row, col, diag = pl.pallas_call(
        kernel,
        out_shape=(
            jax.ShapeDtypeStruct((S, N, COLS), F32),
            jax.ShapeDtypeStruct((S, N, ROWS), F32),
            jax.ShapeDtypeStruct((S, N, N), F32),
        ),
        in_specs=[hbm] * 5,
        out_specs=(hbm, hbm, hbm),
        scratch_shapes=[
            pltpu.SMEM(start_order.shape, jnp.int32),
            pltpu.SMEM(ancestors.shape, jnp.int32),
            pltpu.VMEM((ROWS, COLS), F32),
            pltpu.VMEM((ROWS, COLS), BF),
            pltpu.VMEM((ROWS, COLS), BF),
            pltpu.VMEM((S, N, N), F32),
            pltpu.VMEM((2, S, N, COLS), F32),
            pltpu.VMEM((S, N, N), F32),
            pltpu.VMEM((U, NC, H, ROWS), F32),
            pltpu.VMEM((U, W, ROWS), BF),
            pltpu.VMEM((U, W, ROWS), BF),
            pltpu.VMEM((U, NZ, 2, H, COLS), F32),
            pltpu.VMEM((U, 2, 2, half - 1, H, COLS), F32),
            pltpu.VMEM((U, 2, 2, H, COLS), F32),
            pltpu.VMEM((U, H, COLS), F32),
            pltpu.VMEM((U, H, COLS), F32),
            pltpu.VMEM((S, 128, ROWS), F32),
            pltpu.VMEM((S, NR, 8, 128), F32),
            pltpu.VMEM((S, NR - 1, 8, 128), F32),
            dma((8,)),
            dma((3,)),
            dma((U, chips)),
            dma((U, chips)),
            dma((U,)),
            dma((U,)),
            dma((U, chips)),
            dma((U, 2, 2, half)),
            dma((U, 2, 2, half - 1)),
            dma((U, 2, 2)),
            dma((U,)),
            dma((U,)),
            dma((U,)),
            dma((U,)),
            dma((S, NR - 1)),
            dma((S,)),
        ],
        compiler_params=pltpu.CompilerParams(
            collective_id=0, has_side_effects=True, vmem_limit_bytes=60 * 1024 * 1024
        ),
        name="selected_inverse",
    )(start_order, ancestors, resident_inverse, jnp.swapaxes(factor_panel, 1, 2), diag_inverse)
    row, col, diag = deliver(row, col, diag)
    return jnp.swapaxes(col, 1, 2), row, diag


def solution(mesh):
    return jax.shard_map(
        on_device,
        mesh=mesh,
        in_specs=(P("row", "col"), P(None, "row", "col"), P(None, "row", "col"), P(), P()),
        out_specs=(P(None, "row", "col"), P(None, "row", "col"), P(None, "row", "col")),
        check_vma=False,
    )
```

```python
import jax
import jax.numpy as jnp
from jax import lax
from jax.experimental import pallas as pl
from jax.experimental.pallas import tpu as pltpu
from jax.sharding import PartitionSpec as P

MESH = pl.DeviceIdType.MESH
BF = jnp.bfloat16
F32 = jnp.float32
TILE = 256
S = 2
U = 4
NR = 16
NC = 16
NZ = 8
NY = 4
ROWS = 768
COLS = 768
TILES = ROWS // TILE
N = 16
H = 8
V = NC // 2
W = V * H
CHIPS = [(2, 1), (1, 1), (3, 1), (2, 0), (0, 1), (1, 0), (3, 0)]
CHAINS = [(1, 0), (-1, 1), (-1, 0), (1, 1)]
ROW_PEERS = sorted(((j // 2, j % 2) for j in range(1, NR)), key=lambda p: -min(p[0], NZ - p[0]) - p[1])


def split(x):
    hi = x.astype(BF)
    lo = (x - hi.astype(F32)).astype(BF)
    return hi, lo


def hops(d, g):
    return NZ // 2 if (d == 1) == (g == 0) else NZ // 2 - 1


def kernel(
    order_hbm, anc_hbm, a_hbm, p_hbm, dinv_hbm,
    row_ref, col_ref, diag_ref,
    order, anc, a_buf, a_hi, a_lo, dinv, outs, diags, pt, p_hi, p_lo, t, rp, fin, rows, m, dp, dr,
    local_sem, out_sem, a_send, a_recv, ag_send, ag_recv, fw_send, fw_recv,
    rs_send, rs_recv, fin_recv, x_send, x_recv, m_send, m_recv, d_send, d_recv,
):
    r = lax.axis_index("row")
    c = lax.axis_index("col")
    z, xl = r // 2, r % 2
    y, xh, k = c // 4, (c // 2) % 2, c % 2
    off_diagonal = r != c

    def chip_at(dy, dx):
        return ((y + dy) % NY) * 2 + (xh + dx) % 2

    def row_at(dz, dx):
        return ((z + dz) % NZ) * 2 + (xl + dx) % 2

    sibling = (r, c + 1 - 2 * k)
    barrier = pltpu.get_barrier_semaphore()
    greeted = [(r, chip_at(dy, dx) * 2 + k) for dy, dx in CHIPS]
    for dz, dx in ((1, 0), (1, 1), (-1, 0), (-1, 1), (0, 1)):
        greeted += [(row_at(dz, dx), c), (row_at(dz, dx), c + 1 - 2 * k)]
    greeted.append(sibling)
    for device in greeted:
        pl.semaphore_signal(barrier, inc=1, device_id=device, device_id_type=MESH)

    locals_ = [
        pltpu.make_async_copy(a_hbm, a_buf.at[k], local_sem.at[0]),
        pltpu.make_async_copy(anc_hbm, anc, local_sem.at[1]),
        pltpu.make_async_copy(order_hbm, order, local_sem.at[2]),
        pltpu.make_async_copy(dinv_hbm, dinv, local_sem.at[3]),
    ]
    for u in range(U):
        mine = p_hbm.at[u // 2, pl.ds(u % 2 * H, H)]
        locals_.append(pltpu.make_async_copy(mine, pt.at[u, k, c // 2], local_sem.at[4 + u]))
    for copy in locals_:
        copy.start()
    pl.semaphore_wait(barrier, len(greeted))

    sent = []

    def remote(src, dst, send, recv, device):
        return pltpu.make_async_remote_copy(
            src_ref=src, dst_ref=dst, send_sem=send, recv_sem=recv, device_id=device, device_id_type=MESH
        )

    def send(*args):
        copy = remote(*args)
        copy.start()
        sent.append(copy)

    def settle():
        for copy in sent:
            copy.wait_send()
        sent.clear()

    def spread(u):
        mine = p_hbm.at[u // 2, pl.ds(u % 2 * H, H)]
        for i, (dy, dx) in enumerate(CHIPS):
            there = (r, chip_at(dy, dx) * 2 + k)
            send(mine, pt.at[u, k, c // 2], ag_send.at[u, i], ag_recv.at[u, i], there)

    def mask_and_split(u, core):
        for b in range(TILES):
            here = pl.ds(b * TILE, TILE)
            flag = anc[u // 2, r * TILES + b].astype(F32)
            hi, lo = split(pt[u, core, :, :, here].reshape(W, TILE) * flag)
            p_hi[u, core, :, here] = hi
            p_lo[u, core, :, here] = lo

    def gather(u):
        locals_[4 + u].wait()
        for i, (dy, dx) in list(enumerate(CHIPS))[::-1]:
            there = pt.at[u, k, chip_at(-dy, dx)]
            remote(there, there, ag_send.at[u, i], ag_recv.at[u, i], sibling).wait_recv()
        send(pt.at[u, k], pt.at[u, k], fw_send.at[u], fw_recv.at[u], sibling)
        mask_and_split(u, k)

    def multiply(u, core):
        for b in range(TILES):
            here = pl.ds(b * TILE, TILE)
            v, w = a_hi[core, :, here], a_lo[core, :, here]
            total = jnp.dot(p_hi[u, k], v, preferred_element_type=F32)
            total += jnp.dot(p_hi[u, k], w, preferred_element_type=F32)
            total += jnp.dot(p_lo[u, k], v, preferred_element_type=F32)
            t[u, core, :, :, here] = total.reshape(NZ, H, TILE)

    def other_half(u):
        there = pt.at[u, 1 - k]
        remote(there, there, fw_send.at[u], fw_recv.at[u], sibling).wait_recv()
        mask_and_split(u, 1 - k)

    def side(d):
        return 0 if d == 1 else 1

    def stay(core):
        return jnp.logical_and(xl == k, core == k)

    def own(u, core):
        there = (z * 2 + k, c - k + core)
        return remote(t.at[u, core, z], fin.at[u, 4 + xl], x_send.at[u, core], x_recv.at[u, xl], there)

    def hop(u, j):
        for d, core in CHAINS:
            last = hops(d, core) - 1
            if j > last:
                continue
            e = side(d)
            block = t.at[u, core, (z + d * (last + 1 - j)) % NZ]
            if j == 0:
                src = block
            else:
                src = rp.at[u, e, core, j - 1]
                remote(src, src, rs_send.at[u, e, core, j - 1], rs_recv.at[u, e, core, j - 1], sibling).wait_recv()
                src[...] += block[...]
            if j == last:
                there = (((z + d) % NZ) * 2 + k, c - k + core)
                send(src, fin.at[u, 2 * e + xl], rs_send.at[u, e, core, j], fin_recv.at[u], there)
            else:
                there = (row_at(d, 0), c)
                send(src, rp.at[u, e, core, j], rs_send.at[u, e, core, j], rs_recv.at[u, e, core, j], there)
        if j == 0:
            for core in range(2):

                @pl.when(stay(core))
                def _():
                    fin[u, 4 + xl] = t[u, core, z]

                @pl.when(jnp.logical_not(stay(core)))
                def _():
                    own(u, core).start()

    def mirror(u):
        there = m.at[u // 2, pl.ds(u % 2 * H, H)]
        return remote(rows.at[u], there, m_send.at[u], m_recv.at[u], (c, r))

    def finish(u):
        for x in range(2):

            @pl.when(jnp.logical_not(jnp.logical_and(xl == k, xl == x)))
            def _():
                there = fin.at[u, 4 + x]
                remote(there, there, x_send.at[u, 0], x_recv.at[u, x], sibling).wait_recv()

        there = fin.at[u, pl.ds(0, 4)]
        remote(there, there, rs_send.at[u, 0, 0, 0], fin_recv.at[u], sibling).wait_recv()
        for b in range(TILES):
            here = pl.ds(b * TILE, TILE)
            total = fin[u, 4, :, here] + fin[u, 5, :, here]
            total += fin[u, 0, :, here] + fin[u, 1, :, here]
            total += fin[u, 2, :, here] + fin[u, 3, :, here]
            rows[u, :, here] = total * -anc[u // 2, c * TILES + b].astype(F32)

        @pl.when(off_diagonal)
        def _():
            mirror(u).start()

        @pl.when(jnp.logical_not(off_diagonal))
        def _():
            m[u // 2, pl.ds(u % 2 * H, H), :] = rows[u]

    def diagonal(s):
        for h in range(2):

            @pl.when(off_diagonal)
            def _():
                mirror(2 * s + h).wait_recv()

        v, w = split(m[s])
        halves = []
        for h in range(2):
            total = jnp.zeros((2 * W, 128), F32)
            for left, right in ((p_hi, v), (p_hi, w), (p_lo, v)):
                panel = left[2 * s + h].reshape(2 * W, ROWS)
                total += lax.dot_general(panel, right, (((1,), (1,)), ((), ())), preferred_element_type=F32)
            halves.append(total)
        dp[s] = (halves[0] + pltpu.roll(halves[1], N, 1)).reshape(2, NZ, 8, 128)
        for i, (dz, dx) in enumerate(ROW_PEERS):
            part = dp.at[s, (xl + dx) % 2, (z + dz) % NZ]
            send(part, dr.at[s, i], d_send.at[s, i], d_recv.at[s], (row_at(dz, dx), c))

    def add_diagonal(s):
        total = dp[s, xl, z]
        remote(dr.at[s], dr.at[s], d_send.at[s, 0], d_recv.at[s], sibling).wait_recv()
        for i in range(NR - 1):
            total += dr[s, i]
        return total

    def split_inverse(core):
        for b in range(TILES):
            here = pl.ds(b * TILE, TILE)
            hi, lo = split(a_buf[core, here, :])
            a_hi[core, here, :] = hi
            a_lo[core, here, :] = lo

    spread(0)
    spread(1)
    spread(2)
    spread(3)
    send(a_hbm, a_buf.at[k], a_send, a_recv, sibling)
    m[:, pl.ds(N, 128 - N), :] = jnp.zeros((S, 128 - N, ROWS), F32)
    locals_[0].wait()
    split_inverse(k)
    locals_[1].wait()
    remote(a_hbm, a_buf.at[1 - k], a_send, a_recv, sibling).wait_recv()
    split_inverse(1 - k)
    gather(0)
    multiply(0, 0)
    multiply(0, 1)
    hop(0, 0)
    gather(1)
    multiply(1, 0)
    multiply(1, 1)
    hop(1, 0)
    gather(2)
    multiply(2, 0)
    multiply(2, 1)
    hop(0, 1)
    hop(2, 0)
    gather(3)
    multiply(3, 0)
    multiply(3, 1)
    hop(1, 1)
    hop(3, 0)
    other_half(0)
    hop(0, 2)
    hop(2, 1)
    other_half(1)
    hop(1, 2)
    hop(3, 1)
    hop(0, 3)
    other_half(2)
    hop(2, 2)
    hop(1, 3)
    other_half(3)
    hop(3, 2)
    finish(0)
    hop(2, 3)
    finish(1)
    hop(3, 3)
    finish(2)
    finish(3)
    for u in range(U):
        for core in range(2):

            @pl.when(jnp.logical_not(stay(core)))
            def _():
                own(u, core).wait_send()

    settle()
    diagonal(0)
    diagonal(1)
    for u in range(U):

        @pl.when(off_diagonal)
        def _(u=u):
            mirror(u).wait_send()

    for copy in locals_[2:4]:
        copy.wait()
    in_place = order[0] == 0
    for s in range(S):
        outs[0, s] = jnp.where(in_place, m[s, pl.ds(0, N), :], m[1 - s, pl.ds(0, N), :])
        for h in range(2):
            outs[1, s, pl.ds(h * H, H), :] = jnp.where(in_place, rows[2 * s + h], rows[2 - 2 * s + h])
    stores = [
        pltpu.make_async_copy(outs.at[0], col_ref, out_sem.at[0]),
        pltpu.make_async_copy(outs.at[1], row_ref, out_sem.at[1]),
        pltpu.make_async_copy(diags, diag_ref, out_sem.at[2]),
    ]
    stores[0].start()
    stores[1].start()
    settle()
    totals = [add_diagonal(s) for s in range(S)]
    for s in range(S):
        total = jnp.where(in_place, totals[s], totals[1 - s])
        for h in range(2):
            chosen = jnp.where(in_place, dinv[s, pl.ds(h * H, H)], dinv[1 - s, pl.ds(h * H, H)])
            diags[s, pl.ds(h * H, H), :] = chosen - total[:, h * N : (h + 1) * N]
    stores[2].start()
    for copy in stores:
        copy.wait()


def copy_out(*refs):
    for i in range(3):
        refs[3 + i][...] = refs[i][...]


def deliver(*arrays):
    return pl.pallas_call(
        copy_out,
        out_shape=tuple(jax.ShapeDtypeStruct(x.shape, x.dtype) for x in arrays),
        in_specs=[pl.BlockSpec(memory_space=pltpu.VMEM)] * 3,
        out_specs=(pl.BlockSpec(memory_space=pltpu.VMEM),) * 3,
        scratch_shapes=[pltpu.VMEM(x.shape, x.dtype) for x in arrays] + [pltpu.SemaphoreType.DMA((6,))],
        name="deliver",
    )(*arrays)


def on_device(resident_inverse, factor_panel, diag_inverse, ancestors, start_order):
    hbm = pl.BlockSpec(memory_space=pltpu.HBM)
    dma = pltpu.SemaphoreType.DMA
    half = NZ // 2
    chips = len(CHIPS)
    row, col, diag = pl.pallas_call(
        kernel,
        out_shape=(
            jax.ShapeDtypeStruct((S, N, COLS), F32),
            jax.ShapeDtypeStruct((S, N, ROWS), F32),
            jax.ShapeDtypeStruct((S, N, N), F32),
        ),
        in_specs=[hbm] * 5,
        out_specs=(hbm, hbm, hbm),
        scratch_shapes=[
            pltpu.SMEM(start_order.shape, jnp.int32),
            pltpu.SMEM(ancestors.shape, jnp.int32),
            pltpu.VMEM((2, ROWS, COLS), F32),
            pltpu.VMEM((2, ROWS, COLS), BF),
            pltpu.VMEM((2, ROWS, COLS), BF),
            pltpu.VMEM((S, N, N), F32),
            pltpu.VMEM((2, S, N, COLS), F32),
            pltpu.VMEM((S, N, N), F32),
            pltpu.VMEM((U, 2, V, H, ROWS), F32),
            pltpu.VMEM((U, 2, W, ROWS), BF),
            pltpu.VMEM((U, 2, W, ROWS), BF),
            pltpu.VMEM((U, 2, NZ, H, COLS), F32),
            pltpu.VMEM((U, 2, 2, half - 1, H, COLS), F32),
            pltpu.VMEM((U, 6, H, COLS), F32),
            pltpu.VMEM((U, H, COLS), F32),
            pltpu.VMEM((S, 128, ROWS), F32),
            pltpu.VMEM((S, 2, NZ, 8, 128), F32),
            pltpu.VMEM((S, NR - 1, 8, 128), F32),
            dma((8,)),
            dma((3,)),
            dma,
            dma,
            dma((U, chips)),
            dma((U, chips)),
            dma((U,)),
            dma((U,)),
            dma((U, 2, 2, half)),
            dma((U, 2, 2, half - 1)),
            dma((U,)),
            dma((U, 2)),
            dma((U, 2)),
            dma((U,)),
            dma((U,)),
            dma((S, NR - 1)),
            dma((S,)),
        ],
        compiler_params=pltpu.CompilerParams(
            collective_id=0, has_side_effects=True, vmem_limit_bytes=60 * 1024 * 1024
        ),
        name="selected_inverse",
    )(start_order, ancestors, resident_inverse, jnp.swapaxes(factor_panel, 1, 2), diag_inverse)
    row, col, diag = deliver(row, col, diag)
    return jnp.swapaxes(col, 1, 2), row, diag


def solution(mesh):
    return jax.shard_map(
        on_device,
        mesh=mesh,
        in_specs=(P("row", "col"), P(None, "row", "col"), P(None, "row", "col"), P(), P()),
        out_specs=(P(None, "row", "col"), P(None, "row", "col"), P(None, "row", "col")),
        check_vma=False,
    )
```

```python
import jax
import jax.numpy as jnp
from jax import lax
from jax.experimental import pallas as pl
from jax.experimental.pallas import tpu as pltpu
from jax.sharding import PartitionSpec as P

MESH = pl.DeviceIdType.MESH
BF = jnp.bfloat16
F32 = jnp.float32
TILE = 256
S = 2
U = 4
NR = 16
NC = 16
NZ = 8
NY = 4
ROWS = 768
COLS = 768
TILES = ROWS // TILE
N = 16
H = 8
V = NC // 2
W = V * H
CHIPS = [(2, 1), (1, 1), (3, 1), (2, 0), (0, 1), (1, 0), (3, 0)]
CHAINS = [(1, 0), (-1, 1), (-1, 0), (1, 1)]
ROW_PEERS = sorted(((j // 2, j % 2) for j in range(1, NR)), key=lambda p: -min(p[0], NZ - p[0]) - p[1])


def split(x):
    hi = x.astype(BF)
    lo = (x - hi.astype(F32)).astype(BF)
    return hi, lo


def hops(d, g):
    return NZ // 2 if (d == 1) == (g == 0) else NZ // 2 - 1


def kernel(
    order_hbm, anc_hbm, a_hbm, p_hbm, dinv_hbm,
    row_ref, col_ref, diag_ref,
    order, anc, a_buf, a_hi, a_lo, dinv, outs, diags, pt, p_hi, p_lo, t, rp, fin, rows, m, dp, dr,
    local_sem, out_sem, a_send, a_recv, ag_send, ag_recv, fw_send, fw_recv,
    rs_send, rs_recv, fin_recv, x_send, x_recv, m_send, m_recv, d_send, d_recv,
):
    r = lax.axis_index("row")
    c = lax.axis_index("col")
    z, xl = r // 2, r % 2
    y, xh, k = c // 4, (c // 2) % 2, c % 2
    off_diagonal = r != c

    def chip_at(dy, dx):
        return ((y + dy) % NY) * 2 + (xh + dx) % 2

    def row_at(dz, dx):
        return ((z + dz) % NZ) * 2 + (xl + dx) % 2

    sibling = (r, c + 1 - 2 * k)
    barrier = pltpu.get_barrier_semaphore()
    greeted = [(r, chip_at(dy, dx) * 2 + k) for dy, dx in CHIPS]
    for dz, dx in ((1, 0), (1, 1), (-1, 0), (-1, 1), (0, 1)):
        greeted += [(row_at(dz, dx), c), (row_at(dz, dx), c + 1 - 2 * k)]
    greeted.append(sibling)
    for device in greeted:
        pl.semaphore_signal(barrier, inc=1, device_id=device, device_id_type=MESH)

    locals_ = [
        pltpu.make_async_copy(a_hbm, a_buf.at[k], local_sem.at[0]),
        pltpu.make_async_copy(anc_hbm, anc, local_sem.at[1]),
        pltpu.make_async_copy(order_hbm, order, local_sem.at[2]),
        pltpu.make_async_copy(dinv_hbm, dinv, local_sem.at[3]),
    ]
    for u in range(U):
        mine = p_hbm.at[u // 2, pl.ds(u % 2 * H, H)]
        locals_.append(pltpu.make_async_copy(mine, pt.at[u, k, c // 2], local_sem.at[4 + u]))
    for copy in locals_:
        copy.start()
    pl.semaphore_wait(barrier, len(greeted))

    sent = []

    def remote(src, dst, send, recv, device):
        return pltpu.make_async_remote_copy(
            src_ref=src, dst_ref=dst, send_sem=send, recv_sem=recv, device_id=device, device_id_type=MESH
        )

    def send(*args):
        copy = remote(*args)
        copy.start()
        sent.append(copy)

    def settle():
        for copy in sent:
            copy.wait_send()
        sent.clear()

    def spread(u):
        mine = p_hbm.at[u // 2, pl.ds(u % 2 * H, H)]
        for i, (dy, dx) in enumerate(CHIPS):
            there = (r, chip_at(dy, dx) * 2 + k)
            send(mine, pt.at[u, k, c // 2], ag_send.at[u, i], ag_recv.at[u, i], there)

    def mask_and_split(u, core):
        for b in range(TILES):
            here = pl.ds(b * TILE, TILE)
            flag = anc[u // 2, r * TILES + b].astype(F32)
            hi, lo = split(pt[u, core, :, :, here].reshape(W, TILE) * flag)
            p_hi[u, core, :, here] = hi
            p_lo[u, core, :, here] = lo

    def gather(u):
        locals_[4 + u].wait()
        for i, (dy, dx) in list(enumerate(CHIPS))[::-1]:
            there = pt.at[u, k, chip_at(-dy, dx)]
            remote(there, there, ag_send.at[u, i], ag_recv.at[u, i], sibling).wait_recv()
        send(pt.at[u, k], pt.at[u, k], fw_send.at[u], fw_recv.at[u], sibling)
        mask_and_split(u, k)

    def multiply(u, core):
        for b in range(TILES):
            here = pl.ds(b * TILE, TILE)
            v, w = a_hi[core, :, here], a_lo[core, :, here]
            total = jnp.dot(p_hi[u, k], v, preferred_element_type=F32)
            total += jnp.dot(p_hi[u, k], w, preferred_element_type=F32)
            total += jnp.dot(p_lo[u, k], v, preferred_element_type=F32)
            t[u, core, :, :, here] = total.reshape(NZ, H, TILE)

    def other_half(u):
        there = pt.at[u, 1 - k]
        remote(there, there, fw_send.at[u], fw_recv.at[u], sibling).wait_recv()
        mask_and_split(u, 1 - k)

    def side(d):
        return 0 if d == 1 else 1

    def stay(core):
        return jnp.logical_and(xl == k, core == k)

    def own(u, core):
        there = (z * 2 + k, c - k + core)
        return remote(t.at[u, core, z], fin.at[u, 4 + xl], x_send.at[u, core], x_recv.at[u, xl], there)

    def hop(u, j):
        for d, core in CHAINS:
            last = hops(d, core) - 1
            if j > last:
                continue
            e = side(d)
            block = t.at[u, core, (z + d * (last + 1 - j)) % NZ]
            if j == 0:
                src = block
            else:
                src = rp.at[u, e, core, j - 1]
                remote(src, src, rs_send.at[u, e, core, j - 1], rs_recv.at[u, e, core, j - 1], sibling).wait_recv()
                src[...] += block[...]
            if j == last:
                there = (((z + d) % NZ) * 2 + k, c - k + core)
                send(src, fin.at[u, 2 * e + xl], rs_send.at[u, e, core, j], fin_recv.at[u], there)
            else:
                there = (row_at(d, 0), c)
                send(src, rp.at[u, e, core, j], rs_send.at[u, e, core, j], rs_recv.at[u, e, core, j], there)
        if j == 0:
            for core in range(2):

                @pl.when(stay(core))
                def _():
                    fin[u, 4 + xl] = t[u, core, z]

                @pl.when(jnp.logical_not(stay(core)))
                def _():
                    own(u, core).start()

    def mirror(u):
        there = m.at[u // 2, pl.ds(u % 2 * H, H)]
        return remote(rows.at[u], there, m_send.at[u], m_recv.at[u], (c, r))

    def finish(u):
        for x in range(2):

            @pl.when(jnp.logical_not(jnp.logical_and(xl == k, xl == x)))
            def _():
                there = fin.at[u, 4 + x]
                remote(there, there, x_send.at[u, 0], x_recv.at[u, x], sibling).wait_recv()

        there = fin.at[u, pl.ds(0, 4)]
        remote(there, there, rs_send.at[u, 0, 0, 0], fin_recv.at[u], sibling).wait_recv()
        for b in range(TILES):
            here = pl.ds(b * TILE, TILE)
            total = fin[u, 4, :, here] + fin[u, 5, :, here]
            total += fin[u, 0, :, here] + fin[u, 1, :, here]
            total += fin[u, 2, :, here] + fin[u, 3, :, here]
            rows[u, :, here] = total * -anc[u // 2, c * TILES + b].astype(F32)


    def reflect(u):
        @pl.when(off_diagonal)
        def _():
            mirror(u).start()

        @pl.when(jnp.logical_not(off_diagonal))
        def _():
            m[u // 2, pl.ds(u % 2 * H, H), :] = rows[u]

    def diagonal(s):
        for h in range(2):

            @pl.when(off_diagonal)
            def _():
                mirror(2 * s + h).wait_recv()

        v, w = split(m[s])
        halves = []
        for h in range(2):
            total = jnp.zeros((2 * W, 128), F32)
            for left, right in ((p_hi, v), (p_hi, w), (p_lo, v)):
                panel = left[2 * s + h].reshape(2 * W, ROWS)
                total += lax.dot_general(panel, right, (((1,), (1,)), ((), ())), preferred_element_type=F32)
            halves.append(total)
        dp[s] = (halves[0] + pltpu.roll(halves[1], N, 1)).reshape(2, NZ, 8, 128)
        for i, (dz, dx) in enumerate(ROW_PEERS):
            part = dp.at[s, (xl + dx) % 2, (z + dz) % NZ]
            send(part, dr.at[s, i], d_send.at[s, i], d_recv.at[s], (row_at(dz, dx), c))

    def add_diagonal(s):
        total = dp[s, xl, z]
        remote(dr.at[s], dr.at[s], d_send.at[s, 0], d_recv.at[s], sibling).wait_recv()
        for i in range(NR - 1):
            total += dr[s, i]
        return total

    def split_inverse(core):
        for b in range(TILES):
            here = pl.ds(b * TILE, TILE)
            hi, lo = split(a_buf[core, here, :])
            a_hi[core, here, :] = hi
            a_lo[core, here, :] = lo

    spread(0)
    spread(1)
    spread(2)
    spread(3)
    send(a_hbm, a_buf.at[k], a_send, a_recv, sibling)
    m[:, pl.ds(N, 128 - N), :] = jnp.zeros((S, 128 - N, ROWS), F32)
    locals_[0].wait()
    split_inverse(k)
    locals_[1].wait()
    remote(a_hbm, a_buf.at[1 - k], a_send, a_recv, sibling).wait_recv()
    split_inverse(1 - k)
    gather(0)
    multiply(0, 0)
    multiply(0, 1)
    hop(0, 0)
    gather(1)
    multiply(1, 0)
    multiply(1, 1)
    hop(1, 0)
    gather(2)
    multiply(2, 0)
    multiply(2, 1)
    hop(0, 1)
    hop(2, 0)
    gather(3)
    multiply(3, 0)
    multiply(3, 1)
    hop(1, 1)
    hop(3, 0)
    other_half(0)
    hop(0, 2)
    hop(2, 1)
    other_half(1)
    hop(1, 2)
    hop(3, 1)
    hop(0, 3)
    other_half(2)
    hop(2, 2)
    hop(1, 3)
    other_half(3)
    hop(3, 2)
    finish(0)
    reflect(0)
    hop(2, 3)
    finish(1)
    hop(3, 3)
    reflect(1)
    finish(2)
    reflect(2)
    finish(3)
    reflect(3)
    for u in range(U):
        for core in range(2):

            @pl.when(jnp.logical_not(stay(core)))
            def _():
                own(u, core).wait_send()

    settle()
    diagonal(0)
    diagonal(1)
    for u in range(U):

        @pl.when(off_diagonal)
        def _(u=u):
            mirror(u).wait_send()

    for copy in locals_[2:4]:
        copy.wait()
    in_place = order[0] == 0
    for s in range(S):
        outs[0, s] = jnp.where(in_place, m[s, pl.ds(0, N), :], m[1 - s, pl.ds(0, N), :])
        for h in range(2):
            outs[1, s, pl.ds(h * H, H), :] = jnp.where(in_place, rows[2 * s + h], rows[2 - 2 * s + h])
    stores = [
        pltpu.make_async_copy(outs.at[0], col_ref, out_sem.at[0]),
        pltpu.make_async_copy(outs.at[1], row_ref, out_sem.at[1]),
        pltpu.make_async_copy(diags, diag_ref, out_sem.at[2]),
    ]
    stores[0].start()
    stores[1].start()
    settle()
    totals = [add_diagonal(s) for s in range(S)]
    for s in range(S):
        total = jnp.where(in_place, totals[s], totals[1 - s])
        for h in range(2):
            chosen = jnp.where(in_place, dinv[s, pl.ds(h * H, H)], dinv[1 - s, pl.ds(h * H, H)])
            diags[s, pl.ds(h * H, H), :] = chosen - total[:, h * N : (h + 1) * N]
    stores[2].start()
    for copy in stores:
        copy.wait()


def copy_out(*refs):
    for i in range(3):
        refs[3 + i][...] = refs[i][...]


def deliver(*arrays):
    return pl.pallas_call(
        copy_out,
        out_shape=tuple(jax.ShapeDtypeStruct(x.shape, x.dtype) for x in arrays),
        in_specs=[pl.BlockSpec(memory_space=pltpu.VMEM)] * 3,
        out_specs=(pl.BlockSpec(memory_space=pltpu.VMEM),) * 3,
        scratch_shapes=[pltpu.VMEM(x.shape, x.dtype) for x in arrays] + [pltpu.SemaphoreType.DMA((6,))],
        name="deliver",
    )(*arrays)


def on_device(resident_inverse, factor_panel, diag_inverse, ancestors, start_order):
    hbm = pl.BlockSpec(memory_space=pltpu.HBM)
    dma = pltpu.SemaphoreType.DMA
    half = NZ // 2
    chips = len(CHIPS)
    row, col, diag = pl.pallas_call(
        kernel,
        out_shape=(
            jax.ShapeDtypeStruct((S, N, COLS), F32),
            jax.ShapeDtypeStruct((S, N, ROWS), F32),
            jax.ShapeDtypeStruct((S, N, N), F32),
        ),
        in_specs=[hbm] * 5,
        out_specs=(hbm, hbm, hbm),
        scratch_shapes=[
            pltpu.SMEM(start_order.shape, jnp.int32),
            pltpu.SMEM(ancestors.shape, jnp.int32),
            pltpu.VMEM((2, ROWS, COLS), F32),
            pltpu.VMEM((2, ROWS, COLS), BF),
            pltpu.VMEM((2, ROWS, COLS), BF),
            pltpu.VMEM((S, N, N), F32),
            pltpu.VMEM((2, S, N, COLS), F32),
            pltpu.VMEM((S, N, N), F32),
            pltpu.VMEM((U, 2, V, H, ROWS), F32),
            pltpu.VMEM((U, 2, W, ROWS), BF),
            pltpu.VMEM((U, 2, W, ROWS), BF),
            pltpu.VMEM((U, 2, NZ, H, COLS), F32),
            pltpu.VMEM((U, 2, 2, half - 1, H, COLS), F32),
            pltpu.VMEM((U, 6, H, COLS), F32),
            pltpu.VMEM((U, H, COLS), F32),
            pltpu.VMEM((S, 128, ROWS), F32),
            pltpu.VMEM((S, 2, NZ, 8, 128), F32),
            pltpu.VMEM((S, NR - 1, 8, 128), F32),
            dma((8,)),
            dma((3,)),
            dma,
            dma,
            dma((U, chips)),
            dma((U, chips)),
            dma((U,)),
            dma((U,)),
            dma((U, 2, 2, half)),
            dma((U, 2, 2, half - 1)),
            dma((U,)),
            dma((U, 2)),
            dma((U, 2)),
            dma((U,)),
            dma((U,)),
            dma((S, NR - 1)),
            dma((S,)),
        ],
        compiler_params=pltpu.CompilerParams(
            collective_id=0, has_side_effects=True, vmem_limit_bytes=60 * 1024 * 1024
        ),
        name="selected_inverse",
    )(start_order, ancestors, resident_inverse, jnp.swapaxes(factor_panel, 1, 2), diag_inverse)
    row, col, diag = deliver(row, col, diag)
    return jnp.swapaxes(col, 1, 2), row, diag


def solution(mesh):
    return jax.shard_map(
        on_device,
        mesh=mesh,
        in_specs=(P("row", "col"), P(None, "row", "col"), P(None, "row", "col"), P(), P()),
        out_specs=(P(None, "row", "col"), P(None, "row", "col"), P(None, "row", "col")),
        check_vma=False,
    )
```

```python
import jax
import jax.numpy as jnp
from jax import lax
from jax.experimental import pallas as pl
from jax.experimental.pallas import tpu as pltpu
from jax.sharding import PartitionSpec as P

MESH = pl.DeviceIdType.MESH
BF = jnp.bfloat16
F32 = jnp.float32
TILE = 256
S = 2
U = 4
NR = 16
NC = 16
NZ = 8
NY = 4
ROWS = 768
COLS = 768
TILES = ROWS // TILE
N = 16
H = 8
V = NC // 2
W = V * H
CHIPS = [(2, 1), (1, 1), (3, 1), (2, 0), (0, 1), (1, 0), (3, 0)]
CHAINS = [(1, 0), (-1, 1), (-1, 0), (1, 1)]
ROW_PEERS = sorted(((j // 2, j % 2) for j in range(1, NR)), key=lambda p: -min(p[0], NZ - p[0]) - p[1])


def split(x):
    hi = x.astype(BF)
    lo = (x - hi.astype(F32)).astype(BF)
    return hi, lo


def hops(d, g):
    return NZ // 2 if (d == 1) == (g == 0) else NZ // 2 - 1


def kernel(
    order_hbm, anc_hbm, a_hbm, p_hbm, dinv_hbm,
    row_ref, col_ref, diag_ref,
    order, anc, a_buf, a_hi, a_lo, dinv, outs, diags, pt, p, t, rp, fin, rows, m, dp, dr,
    local_sem, out_sem, a_send, a_recv, ag_send, ag_recv, fw_send, fw_recv,
    rs_send, rs_recv, fin_recv, x_send, x_recv, m_send, m_recv, d_send, d_recv,
):
    r = lax.axis_index("row")
    c = lax.axis_index("col")
    z, xl = r // 2, r % 2
    y, xh, k = c // 4, (c // 2) % 2, c % 2
    off_diagonal = r != c

    def chip_at(dy, dx):
        return ((y + dy) % NY) * 2 + (xh + dx) % 2

    def row_at(dz, dx):
        return ((z + dz) % NZ) * 2 + (xl + dx) % 2

    sibling = (r, c + 1 - 2 * k)
    barrier = pltpu.get_barrier_semaphore()
    greeted = [(r, chip_at(dy, dx) * 2 + k) for dy, dx in CHIPS]
    for dz, dx in ((1, 0), (1, 1), (-1, 0), (-1, 1), (0, 1)):
        greeted += [(row_at(dz, dx), c), (row_at(dz, dx), c + 1 - 2 * k)]
    greeted.append(sibling)
    for device in greeted:
        pl.semaphore_signal(barrier, inc=1, device_id=device, device_id_type=MESH)

    locals_ = [
        pltpu.make_async_copy(a_hbm, a_buf.at[k], local_sem.at[0]),
        pltpu.make_async_copy(anc_hbm, anc, local_sem.at[1]),
        pltpu.make_async_copy(order_hbm, order, local_sem.at[2]),
        pltpu.make_async_copy(dinv_hbm, dinv, local_sem.at[3]),
    ]
    for u in range(U):
        mine = p_hbm.at[u // 2, pl.ds(u % 2 * H, H)]
        locals_.append(pltpu.make_async_copy(mine, pt.at[u, k, c // 2], local_sem.at[4 + u]))
    for copy in locals_:
        copy.start()
    pl.semaphore_wait(barrier, len(greeted))

    sent = []

    def remote(src, dst, send, recv, device):
        return pltpu.make_async_remote_copy(
            src_ref=src, dst_ref=dst, send_sem=send, recv_sem=recv, device_id=device, device_id_type=MESH
        )

    def send(*args):
        copy = remote(*args)
        copy.start()
        sent.append(copy)

    def settle():
        for copy in sent:
            copy.wait_send()
        sent.clear()

    def spread(u):
        mine = p_hbm.at[u // 2, pl.ds(u % 2 * H, H)]
        for i, (dy, dx) in enumerate(CHIPS):
            there = (r, chip_at(dy, dx) * 2 + k)
            send(mine, pt.at[u, k, c // 2], ag_send.at[u, i], ag_recv.at[u, i], there)

    def mask_and_split(u, core):
        for b in range(TILES):
            here = pl.ds(b * TILE, TILE)
            flag = anc[u // 2, r * TILES + b].astype(F32)
            hi, lo = split(pt[u, core, :, :, here].reshape(W, TILE) * flag)
            p[u, core, 0, :, here] = hi
            p[u, core, 1, :, here] = lo

    def gather(u):
        locals_[4 + u].wait()
        for i, (dy, dx) in list(enumerate(CHIPS))[::-1]:
            there = pt.at[u, k, chip_at(-dy, dx)]
            remote(there, there, ag_send.at[u, i], ag_recv.at[u, i], sibling).wait_recv()
        send(pt.at[u, k], pt.at[u, k], fw_send.at[u], fw_recv.at[u], sibling)
        mask_and_split(u, k)

    def multiply(u, core):
        for b in range(TILES):
            here = pl.ds(b * TILE, TILE)
            v, w = a_hi[core, :, here], a_lo[core, :, here]
            both = jnp.dot(p[u, k].reshape(2 * W, ROWS), v, preferred_element_type=F32)
            total = jnp.dot(p[u, k, 0], w, preferred_element_type=F32)
            total += both[:W] + both[W:]
            t[u, core, :, :, here] = total.reshape(NZ, H, TILE)

    def other_half(u):
        there = pt.at[u, 1 - k]
        remote(there, there, fw_send.at[u], fw_recv.at[u], sibling).wait_recv()
        mask_and_split(u, 1 - k)

    def side(d):
        return 0 if d == 1 else 1

    def stay(core):
        return jnp.logical_and(xl == k, core == k)

    def own(u, core):
        there = (z * 2 + k, c - k + core)
        return remote(t.at[u, core, z], fin.at[u, 4 + xl], x_send.at[u, core], x_recv.at[u, xl], there)

    def hop(u, j):
        for d, core in CHAINS:
            last = hops(d, core) - 1
            if j > last:
                continue
            e = side(d)
            block = t.at[u, core, (z + d * (last + 1 - j)) % NZ]
            if j == 0:
                src = block
            else:
                src = rp.at[u, e, core, j - 1]
                remote(src, src, rs_send.at[u, e, core, j - 1], rs_recv.at[u, e, core, j - 1], sibling).wait_recv()
                src[...] += block[...]
            if j == last:
                there = (((z + d) % NZ) * 2 + k, c - k + core)
                send(src, fin.at[u, 2 * e + xl], rs_send.at[u, e, core, j], fin_recv.at[u], there)
            else:
                there = (row_at(d, 0), c)
                send(src, rp.at[u, e, core, j], rs_send.at[u, e, core, j], rs_recv.at[u, e, core, j], there)
        if j == 0:
            for core in range(2):

                @pl.when(stay(core))
                def _():
                    fin[u, 4 + xl] = t[u, core, z]

                @pl.when(jnp.logical_not(stay(core)))
                def _():
                    own(u, core).start()

    def mirror(u):
        there = m.at[u // 2, pl.ds(u % 2 * H, H)]
        return remote(rows.at[u], there, m_send.at[u], m_recv.at[u], (c, r))

    def finish(u):
        for x in range(2):

            @pl.when(jnp.logical_not(jnp.logical_and(xl == k, xl == x)))
            def _():
                there = fin.at[u, 4 + x]
                remote(there, there, x_send.at[u, 0], x_recv.at[u, x], sibling).wait_recv()

        there = fin.at[u, pl.ds(0, 4)]
        remote(there, there, rs_send.at[u, 0, 0, 0], fin_recv.at[u], sibling).wait_recv()
        for b in range(TILES):
            here = pl.ds(b * TILE, TILE)
            total = fin[u, 4, :, here] + fin[u, 5, :, here]
            total += fin[u, 0, :, here] + fin[u, 1, :, here]
            total += fin[u, 2, :, here] + fin[u, 3, :, here]
            rows[u, :, here] = total * -anc[u // 2, c * TILES + b].astype(F32)


    def reflect(u):
        @pl.when(off_diagonal)
        def _():
            mirror(u).start()

        @pl.when(jnp.logical_not(off_diagonal))
        def _():
            m[u // 2, pl.ds(u % 2 * H, H), :] = rows[u]

    def diagonal(s):
        for h in range(2):

            @pl.when(off_diagonal)
            def _():
                mirror(2 * s + h).wait_recv()

        v, w = split(m[s])
        halves = []
        for h in range(2):
            total = jnp.zeros((2 * W, 128), F32)
            for left, right in ((0, v), (0, w), (1, v)):
                panel = p[2 * s + h, :, left].reshape(2 * W, ROWS)
                total += lax.dot_general(panel, right, (((1,), (1,)), ((), ())), preferred_element_type=F32)
            halves.append(total)
        dp[s] = (halves[0] + pltpu.roll(halves[1], N, 1)).reshape(2, NZ, 8, 128)
        for i, (dz, dx) in enumerate(ROW_PEERS):
            part = dp.at[s, (xl + dx) % 2, (z + dz) % NZ]
            send(part, dr.at[s, i], d_send.at[s, i], d_recv.at[s], (row_at(dz, dx), c))

    def add_diagonal(s):
        total = dp[s, xl, z]
        remote(dr.at[s], dr.at[s], d_send.at[s, 0], d_recv.at[s], sibling).wait_recv()
        for i in range(NR - 1):
            total += dr[s, i]
        return total

    def split_inverse(core):
        for b in range(TILES):
            here = pl.ds(b * TILE, TILE)
            hi, lo = split(a_buf[core, here, :])
            a_hi[core, here, :] = hi
            a_lo[core, here, :] = lo

    spread(0)
    spread(1)
    spread(2)
    spread(3)
    send(a_hbm, a_buf.at[k], a_send, a_recv, sibling)
    m[:, pl.ds(N, 128 - N), :] = jnp.zeros((S, 128 - N, ROWS), F32)
    locals_[0].wait()
    split_inverse(k)
    locals_[1].wait()
    remote(a_hbm, a_buf.at[1 - k], a_send, a_recv, sibling).wait_recv()
    split_inverse(1 - k)
    gather(0)
    multiply(0, 0)
    multiply(0, 1)
    hop(0, 0)
    gather(1)
    multiply(1, 0)
    multiply(1, 1)
    hop(1, 0)
    gather(2)
    multiply(2, 0)
    multiply(2, 1)
    hop(0, 1)
    hop(2, 0)
    gather(3)
    multiply(3, 0)
    multiply(3, 1)
    hop(1, 1)
    hop(3, 0)
    other_half(0)
    hop(0, 2)
    hop(2, 1)
    other_half(1)
    hop(1, 2)
    hop(3, 1)
    hop(0, 3)
    other_half(2)
    hop(2, 2)
    hop(1, 3)
    other_half(3)
    hop(3, 2)
    finish(0)
    reflect(0)
    hop(2, 3)
    finish(1)
    hop(3, 3)
    reflect(1)
    finish(2)
    reflect(2)
    finish(3)
    reflect(3)
    for u in range(U):
        for core in range(2):

            @pl.when(jnp.logical_not(stay(core)))
            def _():
                own(u, core).wait_send()

    settle()
    diagonal(0)
    diagonal(1)
    for u in range(U):

        @pl.when(off_diagonal)
        def _(u=u):
            mirror(u).wait_send()

    for copy in locals_[2:4]:
        copy.wait()
    in_place = order[0] == 0
    for s in range(S):
        outs[0, s] = jnp.where(in_place, m[s, pl.ds(0, N), :], m[1 - s, pl.ds(0, N), :])
        for h in range(2):
            outs[1, s, pl.ds(h * H, H), :] = jnp.where(in_place, rows[2 * s + h], rows[2 - 2 * s + h])
    stores = [
        pltpu.make_async_copy(outs.at[0], col_ref, out_sem.at[0]),
        pltpu.make_async_copy(outs.at[1], row_ref, out_sem.at[1]),
        pltpu.make_async_copy(diags, diag_ref, out_sem.at[2]),
    ]
    stores[0].start()
    stores[1].start()
    settle()
    totals = [add_diagonal(s) for s in range(S)]
    for s in range(S):
        total = jnp.where(in_place, totals[s], totals[1 - s])
        for h in range(2):
            chosen = jnp.where(in_place, dinv[s, pl.ds(h * H, H)], dinv[1 - s, pl.ds(h * H, H)])
            diags[s, pl.ds(h * H, H), :] = chosen - total[:, h * N : (h + 1) * N]
    stores[2].start()
    for copy in stores:
        copy.wait()


def copy_out(*refs):
    for i in range(3):
        refs[3 + i][...] = refs[i][...]


def deliver(*arrays):
    return pl.pallas_call(
        copy_out,
        out_shape=tuple(jax.ShapeDtypeStruct(x.shape, x.dtype) for x in arrays),
        in_specs=[pl.BlockSpec(memory_space=pltpu.VMEM)] * 3,
        out_specs=(pl.BlockSpec(memory_space=pltpu.VMEM),) * 3,
        scratch_shapes=[pltpu.VMEM(x.shape, x.dtype) for x in arrays] + [pltpu.SemaphoreType.DMA((6,))],
        name="deliver",
    )(*arrays)


def on_device(resident_inverse, factor_panel, diag_inverse, ancestors, start_order):
    hbm = pl.BlockSpec(memory_space=pltpu.HBM)
    dma = pltpu.SemaphoreType.DMA
    half = NZ // 2
    chips = len(CHIPS)
    row, col, diag = pl.pallas_call(
        kernel,
        out_shape=(
            jax.ShapeDtypeStruct((S, N, COLS), F32),
            jax.ShapeDtypeStruct((S, N, ROWS), F32),
            jax.ShapeDtypeStruct((S, N, N), F32),
        ),
        in_specs=[hbm] * 5,
        out_specs=(hbm, hbm, hbm),
        scratch_shapes=[
            pltpu.SMEM(start_order.shape, jnp.int32),
            pltpu.SMEM(ancestors.shape, jnp.int32),
            pltpu.VMEM((2, ROWS, COLS), F32),
            pltpu.VMEM((2, ROWS, COLS), BF),
            pltpu.VMEM((2, ROWS, COLS), BF),
            pltpu.VMEM((S, N, N), F32),
            pltpu.VMEM((2, S, N, COLS), F32),
            pltpu.VMEM((S, N, N), F32),
            pltpu.VMEM((U, 2, V, H, ROWS), F32),
            pltpu.VMEM((U, 2, 2, W, ROWS), BF),
            pltpu.VMEM((U, 2, NZ, H, COLS), F32),
            pltpu.VMEM((U, 2, 2, half - 1, H, COLS), F32),
            pltpu.VMEM((U, 6, H, COLS), F32),
            pltpu.VMEM((U, H, COLS), F32),
            pltpu.VMEM((S, 128, ROWS), F32),
            pltpu.VMEM((S, 2, NZ, 8, 128), F32),
            pltpu.VMEM((S, NR - 1, 8, 128), F32),
            dma((8,)),
            dma((3,)),
            dma,
            dma,
            dma((U, chips)),
            dma((U, chips)),
            dma((U,)),
            dma((U,)),
            dma((U, 2, 2, half)),
            dma((U, 2, 2, half - 1)),
            dma((U,)),
            dma((U, 2)),
            dma((U, 2)),
            dma((U,)),
            dma((U,)),
            dma((S, NR - 1)),
            dma((S,)),
        ],
        compiler_params=pltpu.CompilerParams(
            collective_id=0, has_side_effects=True, vmem_limit_bytes=60 * 1024 * 1024
        ),
        name="selected_inverse",
    )(start_order, ancestors, resident_inverse, jnp.swapaxes(factor_panel, 1, 2), diag_inverse)
    row, col, diag = deliver(row, col, diag)
    return jnp.swapaxes(col, 1, 2), row, diag


def solution(mesh):
    return jax.shard_map(
        on_device,
        mesh=mesh,
        in_specs=(P("row", "col"), P(None, "row", "col"), P(None, "row", "col"), P(), P()),
        out_specs=(P(None, "row", "col"), P(None, "row", "col"), P(None, "row", "col")),
        check_vma=False,
    )
```
